32 devices in a mesh: leaf: 4 (over y, x), row: 8 (over z, core).
Axes of the slice: x: 2, y: 2, z: 4, core: 2. Of those that a mesh axis runs over, the one named last changes fastest.
Arguments:
- rhs: bfloat16 [6, 4, 512, 256], P(None, 'leaf', 'row'), may hold values from -6 to 6
- diag_inverse: bfloat16 [4, 6, 512, 512], P('leaf'), as said below
- factor: bfloat16 [4, 58, 512, 512], P('leaf', None, 'row'), as said below
- widths: int32 [6, 4], P(None, 'leaf'), may hold values from 64 to 512, as said below
- structure: int32 [4, 58], P('leaf'), may hold values from 0 to 1, as said below
Outputs:
- forward_solution: bfloat16 [6, 4, 512, 256], P(None, 'leaf', 'row')
- adjoint_solution: bfloat16 [6, 4, 512, 256], P(None, 'leaf', 'row')
The draws below stay inside these ranges and needn't reach their ends.
Inputs may be any that keep to these rules, and one draw needn't show every extreme that they name: `widths`: every draw has a supernode of exactly 512 columns and one of exactly one eighth of 512 columns. `structure`: 1 where the block is present. Each diag_inverse[j, l] is lower triangular with diagonal entries from 0.5 to 1. `factor`: dense blocks of independent entries.
All inputs are finite; a program needn't handle non-finite values.
Results may differ from the reference program's by a relative error of at most 0.017.
Values may be sent and summed in bfloat16 or wider, within the bound.
No kernel may reach another device: no remote copies, remote signals or barrier semaphores. Data moves between devices by JAX's collectives and lax.ppermute only.
A program may use at most 64 MiB of HBM per device.

```python
import math
import jax
import jax.numpy as jnp
import numpy as np
from jax import lax

W = 512
RHS = 256
LEVELS = 6
BLOCKS = 58
N_LEAF = 4


def factor_scales():
    values = []
    for source_level in range(LEVELS):
        for target_level in range(source_level + 1, LEVELS):
            group_span = min(2 ** target_level, N_LEAF)
            values = values + [1.0 / math.sqrt(W * target_level * group_span)] * group_span
    return np.array(values, dtype=np.float32)


def draw_factor(key, part):
    scales = jnp.asarray(factor_scales())

    def one_leaf(leaf_number):
        leaf_key = jax.random.fold_in(key, leaf_number)
        base_draw = jax.random.truncated_normal(leaf_key, -4.0, 4.0, (BLOCKS, W, W), jnp.float32)
        return (base_draw * scales[:, None, None]).astype(jnp.bfloat16)
    return lax.map(one_leaf, jnp.arange(N_LEAF))


def draw_diag_inverse(key, part):
    positions = jnp.arange(W)
    strict = (positions[None, :] < positions[:, None]).astype(jnp.float32)
    identity = (positions[None, :] == positions[:, None]).astype(jnp.float32)

    def one_leaf(leaf_number):
        key_lower, key_diagonal = jax.random.split(jax.random.fold_in(key, leaf_number))
        lower_part = jax.random.truncated_normal(key_lower, -4.0, 4.0, (LEVELS, W, W), jnp.float32)
        diagonal = jax.random.uniform(key_diagonal, (LEVELS, W, 1), jnp.float32, 0.5, 1.0)
        matrix = lower_part * strict * math.sqrt(0.5 / W) + identity * diagonal
        return matrix.astype(jnp.bfloat16)
    return lax.map(one_leaf, jnp.arange(N_LEAF))


def draw_widths(key, part):
    entries = LEVELS * N_LEAF
    key_values, key_wide, key_narrow = jax.random.split(key, 3)
    values = jax.random.randint(key_values, (entries,), W // 8, W + 1)
    widest = jax.random.randint(key_wide, (), 0, entries)
    narrow = (widest + jax.random.randint(key_narrow, (), 1, entries)) % entries
    positions = jnp.arange(entries)
    values = jnp.where(positions == widest, W, values)
    values = jnp.where(positions == narrow, W // 8, values)
    return values.reshape(LEVELS, N_LEAF).astype(jnp.int32)


def draw_structure(key, part):
    key_density, key_entries = jax.random.split(key)
    density = jax.random.randint(key_density, (N_LEAF, 1), 1, 9)
    entries = jax.random.randint(key_entries, (N_LEAF, BLOCKS), 0, 8)
    return (entries < density).astype(jnp.int32)


def levels(key, dims, shards, smallest, high):
    loudness = 1.0
    for dim, parts in shards:
        draws = jax.random.uniform(jax.random.fold_in(jax.random.fold_in(key, 6), dim), (parts,), jnp.float32, smallest / len(shards), high / len(shards))
        loudness = loudness * jnp.repeat(jnp.exp(draws), dims[dim] // parts).reshape((-1,) + (1,) * (len(dims) - 1 - dim))
    return loudness


def scatter_about(own_key, extent, width, reach, cuts=(), held_as=jnp.bfloat16):
    level = levels(own_key, extent, cuts, -0.22, 0.18) if cuts else 1.0
    drawn = jax.random.normal(own_key, extent, jnp.float32) * width * level
    return jnp.minimum(jnp.maximum(drawn, -reach), reach).astype(held_as)


def setup_inputs(seed: int = 0) -> dict:
    keys = jax.random.split(jax.random.key(seed), 6)
    return {
        "rhs": scatter_about(keys[0], (LEVELS, N_LEAF, W, RHS), 1.0, 6.0, ((1, 4), (2, 8))),
        "diag_inverse": draw_diag_inverse(jax.random.fold_in(keys[5], 71), 0),
        "factor": draw_factor(jax.random.fold_in(keys[5], 71), 0),
        "widths": draw_widths(jax.random.fold_in(keys[5], 71), 0),
        "structure": draw_structure(jax.random.fold_in(keys[5], 71), 0),
    }


def group_size(level_now):
    return min(2 ** level_now, N_LEAF)


def block_offsets():
    offset_table = {}
    cursor = 0
    for source_level in range(LEVELS):
        for target_level in range(source_level + 1, LEVELS):
            offset_table[(source_level, target_level)] = cursor
            cursor += group_size(target_level)
    return offset_table


def push_block(items):
    block_group, weight_row, values = items
    product = jnp.einsum("mrc,cn->mrn", block_group.astype(jnp.float32), values.astype(jnp.float32), precision=lax.Precision.HIGHEST)
    return product * weight_row[:, None, None]


def pull_block(items):
    block_group, weight_row, values = items
    weighted = values.astype(jnp.float32) * weight_row[:, None, None]
    return jnp.einsum("mrc,mrn->cn", block_group.astype(jnp.float32), weighted, precision=lax.Precision.HIGHEST)


def reference(rhs, diag_inverse, factor, widths, structure):
    offset_table = block_offsets()
    positions = jnp.arange(W, dtype=jnp.int32)
    row_masks = (positions[None, None, :] < widths[:, :, None]).astype(jnp.float32)[..., None]
    weights = structure.astype(jnp.float32)
    forward = []
    for level_now in range(LEVELS):
        group_span = group_size(level_now)
        updates = jnp.zeros((N_LEAF, W, RHS), jnp.float32)
        for source_level in range(level_now):
            first_block = offset_table[(source_level, level_now)]
            pushed = lax.map(push_block, (factor[:, first_block:first_block + group_span], weights[:, first_block:first_block + group_span], forward[source_level]))
            pushed = pushed.reshape(N_LEAF // group_span, group_span, group_span, W, RHS).sum(axis=1)
            updates = updates + pushed.reshape(N_LEAF, W, RHS)
        residual = (row_masks[level_now] * (rhs[level_now].astype(jnp.float32) - updates)).astype(jnp.bfloat16)
        inverse = diag_inverse[:, level_now].astype(jnp.float32)
        solved = jnp.einsum("irc,icn->irn", inverse, residual.astype(jnp.float32), precision=lax.Precision.HIGHEST)
        forward.append((row_masks[level_now] * solved).astype(jnp.bfloat16))
    adjoint = [None] * LEVELS
    for level_now in reversed(range(LEVELS)):
        pulled = jnp.zeros((N_LEAF, W, RHS), jnp.float32)
        for target_level in range(level_now + 1, LEVELS):
            group_span = group_size(target_level)
            first_block = offset_table[(level_now, target_level)]
            grouped = adjoint[target_level].reshape(N_LEAF // group_span, 1, group_span, W, RHS)
            per_source = jnp.broadcast_to(grouped, (N_LEAF // group_span, group_span, group_span, W, RHS)).reshape(N_LEAF, group_span, W, RHS)
            pulled = pulled + lax.map(pull_block, (factor[:, first_block:first_block + group_span], weights[:, first_block:first_block + group_span], per_source))
        reduced = (row_masks[level_now] * (forward[level_now].astype(jnp.float32) - pulled)).astype(jnp.bfloat16)
        inverse = diag_inverse[:, level_now].astype(jnp.float32)
        solved = jnp.einsum("icr,icn->irn", inverse, reduced.astype(jnp.float32), precision=lax.Precision.HIGHEST)
        adjoint[level_now] = (row_masks[level_now] * solved).astype(jnp.bfloat16)
    return jnp.stack(forward), jnp.stack(adjoint)
```

```python
import jax
import jax.numpy as jnp
from jax import lax
from jax.experimental import pallas as pl
from jax.experimental.pallas import tpu as pltpu
from jax.sharding import PartitionSpec as P


F32 = jnp.float32
BF16 = jnp.bfloat16


def from_partner(x, axis, mask):
    return lax.ppermute(x, axis, [(i, i ^ mask) for i in range(lax.axis_size(axis))])


def group_size(level_now, leaf_count):
    return min(2**level_now, leaf_count)


def block_offsets(levels, leaf_count):
    offset_table = {}
    cursor = 0
    for source_level in range(levels):
        for target_level in range(source_level + 1, levels):
            offset_table[source_level, target_level] = cursor
            cursor += group_size(target_level, leaf_count)
    return offset_table


def dot(left, right):
    return jnp.dot(left, right, preferred_element_type=F32)


def call(body, outs, scalars, arrays, scratch=()):
    whole = pl.BlockSpec(memory_space=pltpu.VMEM)
    return pl.pallas_call(
        body,
        out_shape=[jax.ShapeDtypeStruct(s, d) for s, d in outs],
        in_specs=[pl.BlockSpec(memory_space=pltpu.SMEM)] + [whole] * len(arrays),
        out_specs=[whole] * len(outs),
        scratch_shapes=list(scratch),
    )(scalars, *arrays)


def solve_and_push(scalars, parts, inverse, crit, pending, group):
    rows, columns = parts[0].shape
    full = inverse.shape[0]
    n_parts, n_pend = len(parts), 0 if pending is None else 1
    n_crit = 0 if crit is None else 1

    def body(s, *refs):
        part_refs = refs[:n_parts]
        inv_ref = refs[n_parts]
        crit_ref = refs[n_parts + 1] if n_crit else None
        pend_ref = refs[n_parts + 2] if n_pend else None
        at = n_parts + 1 + n_crit + n_pend
        y_ref = refs[at]
        outs, x_ref = refs[at + 1 : -1], refs[-1]
        chip, width, low = s[0], s[2], s[3]
        for k in range(n_parts):
            place = pl.multiple_of((chip ^ k) * rows, rows)
            x_ref[pl.ds(place, rows), :] = part_refs[k][...]
        keep = lax.broadcasted_iota(jnp.int32, (full, columns), 0) < width
        y = jnp.where(keep, dot(inv_ref[...], x_ref[...]), 0.0).astype(BF16)
        y_ref[...] = y
        for k in range(len(outs)):
            p = low ^ k
            product = dot(crit_ref[p], y)
            if n_pend:
                product = product + pend_ref[p]
            outs[k][...] = product.astype(outs[k].dtype)

    outs = [((full, columns), BF16)]
    if n_crit:
        outs.append(((rows, columns), F32))
        outs += [((rows, columns), BF16)] * (group - 1)
    arrays = list(parts) + [inverse] + [crit] * n_crit + [pending] * n_pend
    return call(body, outs, scalars, arrays, [pltpu.VMEM((full, columns), BF16)])


def push_rest(scalars, y, inverse, blocks, pendings, block_rows, rows):
    full, columns = y.shape
    n = len(blocks)
    fresh = pendings is None

    def body(s, *refs):
        y_ref, inv_ref = refs[:2]
        l_refs = refs[2 : 2 + n]
        p_refs = refs[2 + n : 2 + n + (0 if fresh else n)]
        outs = refs[2 + n + (0 if fresh else n) : -1]
        turned_ref = refs[-1]
        chip, core = s[0], s[1]
        y_now = y_ref[...]
        turned_ref[...] = dot(y_now.T, inv_ref[...]).T
        outs[0][...] = turned_ref[pl.ds(pl.multiple_of(chip * rows, rows), rows), :]
        for slot, who in ((1, core), (2, 1 - core)):
            place = pl.multiple_of((chip * 2 + who) * block_rows, block_rows)
            outs[slot][...] = y_ref[pl.ds(place, block_rows), :]
        for k in range(n):
            count = blocks[k].shape[0]
            product = dot(l_refs[k][...].reshape(count * rows, full), y_now)
            product = product.reshape(count, rows, columns)
            if not fresh:
                product = product + p_refs[k][...]
            outs[3 + k][...] = product

    outs = [((rows, columns), F32), ((block_rows, columns), BF16), ((block_rows, columns), BF16)]
    outs += [((b.shape[0], rows, columns), F32) for b in blocks]
    arrays = [y, inverse] + list(blocks) + ([] if fresh else list(pendings))
    return call(body, outs, scalars, arrays, [pltpu.VMEM((full, columns), F32)])


def pull_level(scalars, gathered, crit, inverse, summed, chips):
    rows, columns = gathered[0].shape
    full = inverse.shape[0]
    n = len(gathered)
    n_sum = 0 if summed is None else 1

    def body(s, *refs):
        g_refs = refs[:n]
        crit_ref, inv_ref = refs[n : n + 2]
        sum_ref = refs[n + 2] if n_sum else None
        outs = refs[n + 2 + n_sum : -2]
        stack_ref, turned_ref = refs[-2:]
        chip, width, low = s[0], s[2], s[3]
        for k in range(n):
            place = pl.multiple_of((low ^ k) * rows, rows)
            stack_ref[pl.ds(place, rows), :] = g_refs[k][...]
        left = stack_ref[...].T
        pulled = dot(left, crit_ref[...].reshape(n * rows, full))
        if n_sum:
            pulled = pulled + sum_ref[...]
        keep = lax.broadcasted_iota(jnp.int32, (columns, full), 1) < width
        pulled = jnp.where(keep, pulled, 0.0).astype(BF16)
        turned_ref[...] = dot(pulled, inv_ref[...]).T
        for k in range(chips):
            place = pl.multiple_of((chip ^ k) * rows, rows)
            outs[k][...] = turned_ref[pl.ds(place, rows), :].astype(outs[k].dtype)

    outs = [((rows, columns), F32)] + [((rows, columns), BF16)] * (chips - 1)
    arrays = list(gathered) + [crit, inverse] + [summed] * n_sum
    scratch = [pltpu.VMEM((n * rows, columns), BF16), pltpu.VMEM((full, columns), F32)]
    return call(body, outs, scalars, arrays, scratch)


def pull_rest(scalars, gathered, blocks, sums):
    rows, columns = gathered[0].shape
    full = blocks[0].shape[2]
    n, m = len(gathered), len(blocks)
    fresh = sums is None

    def body(s, *refs):
        g_refs = refs[:n]
        l_refs = refs[n : n + m]
        s_refs = refs[n + m : n + m + (0 if fresh else m)]
        outs, stack_ref = refs[n + m + (0 if fresh else m) : -1], refs[-1]
        low = s[3]
        for k in range(n):
            place = pl.multiple_of((low ^ k) * rows, rows)
            stack_ref[pl.ds(place, rows), :] = g_refs[k][...]
        left = stack_ref[...].T
        for k in range(m):
            term = dot(left, l_refs[k][...].reshape(n * rows, full))
            if not fresh:
                term = term + s_refs[k][...]
            outs[k][...] = term

    outs = [((columns, full), F32)] * m
    arrays = list(gathered) + list(blocks) + ([] if fresh else list(sums))
    return call(body, outs, scalars, arrays, [pltpu.VMEM((n * rows, columns), BF16)])


def shards(rhs, diag_inverse, factor, widths, structure):
    leaf_count = lax.axis_size("leaf")
    chips = lax.axis_size("row") // 2
    leaf = lax.axis_index("leaf")
    row = lax.axis_index("row")
    chip, core = row // 2, row % 2
    levels, block_rows = rhs.shape[0], rhs.shape[2]
    rows = 2 * block_rows
    half = rhs.shape[3] // 2
    first = core == 0
    offsets = block_offsets(levels, leaf_count)
    widths = widths[:, 0]

    def in_order(mine, theirs, axis):
        return jnp.where(
            first,
            jnp.concatenate([mine, theirs], axis),
            jnp.concatenate([theirs, mine], axis),
        )

    left_half, right_half = rhs[:, 0, :, :half], rhs[:, 0, :, half:]
    rhs_theirs = from_partner(jnp.where(first, right_half, left_half), "row", 1)
    rhs_pair = in_order(jnp.where(first, left_half, right_half), rhs_theirs, 1)
    own_blocks = factor[0]
    their_blocks = from_partner(own_blocks, "row", 1)
    weights = structure[0].astype(BF16)
    block = {}
    for (s, t), at in offsets.items():
        end = at + group_size(t, leaf_count)
        block[s, t] = (
            in_order(own_blocks[at:end], their_blocks[at:end], 1) * weights[at:end, None, None]
        )

    position = chip * rows + jnp.arange(rows, dtype=jnp.int32)[:, None]
    scalars = []
    for l in range(levels):
        group = group_size(min(l + 1, levels - 1), leaf_count)
        scalars.append(jnp.stack([chip, core, widths[l], leaf % group]).astype(jnp.int32))

    def exchange_chips(pieces):
        return [from_partner(piece, "row", 2 * k) for k, piece in enumerate(pieces, 1)]

    def exchange_leaves(pieces):
        return [from_partner(piece, "leaf", k) for k, piece in enumerate(pieces, 1)]

    pending = {t: None for t in range(levels)}
    solved, turned, kept, sent = [], [], [], []
    for l in range(levels):
        update = 0.0
        if l > 0:
            update = partial_own
            for piece in exchange_leaves(messages):
                update = update + piece.astype(F32)
        residual = jnp.where(
            position < widths[l], rhs_pair[l].astype(F32) - update, 0.0
        ).astype(BF16)
        parts = [residual] + exchange_chips([residual] * (chips - 1))
        inverse = diag_inverse[0, l]
        if l + 1 < levels:
            group = group_size(l + 1, leaf_count)
            y, partial_own, *messages = solve_and_push(
                scalars[l], parts, inverse, block[l, l + 1], pending[l + 1], group
            )
        else:
            (y,) = solve_and_push(scalars[l], parts, inverse, None, None, 1)
        later = list(range(l + 2, levels))
        before = None if l == 0 else [pending[t] for t in later]
        turned_now, keep, send, *after = push_rest(
            scalars[l], y, inverse, [block[l, t] for t in later], before, block_rows, rows
        )
        pending.update(zip(later, after))
        solved.append(y)
        turned.append(turned_now)
        kept.append(keep)
        sent.append(send)
    forward = in_order(jnp.stack(kept), from_partner(jnp.stack(sent), "row", 1), 2)

    sums = {l: None for l in range(levels)}
    adjoint = [None] * levels
    for l in reversed(range(levels)):
        value = turned[l]
        if l + 1 < levels:
            own_term, *messages = pull_level(
                scalars[l], gathered, block[l, l + 1], diag_inverse[0, l], sums[l], chips
            )
            total = own_term
            for piece in exchange_chips(messages):
                total = total + piece.astype(F32)
            value = value - total
        now = jnp.where(position < widths[l], value, 0.0).astype(BF16)
        adjoint[l] = now
        if l > 0:
            group = group_size(l, leaf_count)
            gathered = [now] + exchange_leaves([now] * (group - 1))
            sources = list(range(l - 1))
            if sources:
                before = None if l + 1 == levels else [sums[s] for s in sources]
                after = pull_rest(
                    scalars[l - 1], gathered, [block[s, l] for s in sources], before
                )
                sums.update(zip(sources, after))
    stacked = jnp.stack(adjoint)
    low_rows, high_rows = stacked[:, :block_rows], stacked[:, block_rows:]
    theirs = from_partner(jnp.where(first, high_rows, low_rows), "row", 1)
    backward = in_order(jnp.where(first, low_rows, high_rows), theirs, 2)
    return forward[:, None], backward[:, None]


def solution(mesh):
    placed = (
        P(None, "leaf", "row", None),
        P("leaf", None, None, None),
        P("leaf", None, "row", None),
        P(None, "leaf"),
        P("leaf", None),
    )
    return jax.shard_map(
        shards,
        mesh=mesh,
        in_specs=placed,
        out_specs=(P(None, "leaf", "row", None), P(None, "leaf", "row", None)),
        check_vma=False,
    )
```

```python
import jax
import jax.numpy as jnp
from jax import lax
from jax.experimental import pallas as pl
from jax.experimental.pallas import tpu as pltpu
from jax.sharding import PartitionSpec as P


F32 = jnp.float32
BF16 = jnp.bfloat16
VMEM_LIMIT = 12 * 2**20


def from_partner(x, axis, mask):
    return lax.ppermute(x, axis, [(i, i ^ mask) for i in range(lax.axis_size(axis))])


def group_size(level_now, leaf_count):
    return min(2**level_now, leaf_count)


def block_offsets(levels, leaf_count):
    offset_table = {}
    cursor = 0
    for source_level in range(levels):
        for target_level in range(source_level + 1, levels):
            offset_table[source_level, target_level] = cursor
            cursor += group_size(target_level, leaf_count)
    return offset_table


def dot(left, right):
    return jnp.dot(left, right, preferred_element_type=F32)


def call(body, outs, scalars, arrays, scratch=(), name=None, limit=VMEM_LIMIT, anywhere=False):
    vmem = pl.BlockSpec(memory_space=pltpu.VMEM)
    given = pl.BlockSpec(memory_space=pl.ANY) if anywhere else vmem
    return pl.pallas_call(
        body,
        out_shape=[jax.ShapeDtypeStruct(s, d) for s, d in outs],
        in_specs=[pl.BlockSpec(memory_space=pltpu.SMEM)] * len(scalars) + [given] * len(arrays),
        out_specs=[vmem] * len(outs),
        scratch_shapes=list(scratch),
        compiler_params=pltpu.CompilerParams(vmem_limit_bytes=limit),
        name=name,
    )(*scalars, *arrays)


def aligned(index, size):
    return pl.multiple_of(index * size, size)


def assemble(scalars, own, theirs, places, block_rows):
    width = own.shape[2]
    n = len(places)

    def body(s, own_ref, their_ref, *refs):
        outs, sem = refs[:n], refs[n]
        core = s[1]
        copies = []
        for k, (at, count) in enumerate(places):
            for source, who in ((own_ref, core), (their_ref, 1 - core)):
                copies.append(
                    pltpu.make_async_copy(
                        source.at[pl.ds(at, count)],
                        outs[k].at[:, pl.ds(aligned(who, block_rows), block_rows), :],
                        sem.at[len(copies)],
                    )
                )
        for copy in copies:
            copy.start()
        for copy in copies:
            copy.wait()

    outs = [((count, 2 * block_rows, width), BF16) for _, count in places]
    scratch = [pltpu.SemaphoreType.DMA((2 * n,))]
    return call(body, outs, [scalars], [own, theirs], scratch, "assemble", anywhere=True)


def solve_and_push(scalars, level, parts, inverse, crit, pending, group, at):
    rows, columns = parts[0].shape
    full = inverse.shape[0]
    n_parts, n_pend = len(parts), 0 if pending is None else 1
    n_crit = 0 if crit is None else 1

    def body(s, w, *refs):
        part_refs = refs[:n_parts]
        inv_ref = refs[n_parts]
        crit_ref = refs[n_parts + 1] if n_crit else None
        pend_ref = refs[n_parts + 2] if n_pend else None
        out = n_parts + 1 + n_crit + n_pend
        y_ref = refs[out]
        outs, x_ref = refs[out + 1 : -1], refs[-1]
        chip, low, width = s[0], s[2] & (group - 1), s[3 + level]
        for k in range(n_parts):
            x_ref[pl.ds(aligned(chip ^ k, rows), rows), :] = part_refs[k][...]
        keep = lax.broadcasted_iota(jnp.int32, (full, columns), 0) < width
        x = jnp.where(keep, x_ref[...], jnp.zeros((), BF16))
        y = jnp.where(keep, dot(inv_ref[...], x), 0.0).astype(BF16)
        y_ref[...] = y
        for k in range(len(outs)):
            p = low ^ k
            product = dot(crit_ref[p], y) * w[at + p].astype(F32)
            if n_pend:
                product = product + pend_ref[p]
            outs[k][...] = product.astype(outs[k].dtype)

    outs = [((full, columns), BF16)]
    if n_crit:
        outs.append(((rows, columns), F32))
        outs += [((rows, columns), BF16)] * (group - 1)
    arrays = list(parts) + [inverse] + [crit] * n_crit + [pending] * n_pend
    return call(body, outs, scalars, arrays, [pltpu.VMEM((full, columns), BF16)], "solve_and_push")


def push_rest(scalars, level, y, inverse, blocks, pendings, starts, block_rows, rows):
    full, columns = y.shape
    n = len(blocks)
    fresh = pendings is None

    def body(s, w, *refs):
        y_ref, inv_ref = refs[:2]
        l_refs = refs[2 : 2 + n]
        p_refs = refs[2 + n : 2 + n + (0 if fresh else n)]
        outs = refs[2 + n + (0 if fresh else n) : -1]
        turned_ref = refs[-1]
        chip, core, width = s[0], s[1], s[3 + level]
        y_now = y_ref[...]
        keep = lax.broadcasted_iota(jnp.int32, (full, columns), 0) < width
        turned_ref[...] = jnp.where(keep, dot(y_now.T, inv_ref[...]).T, 0.0)
        outs[0][...] = turned_ref[pl.ds(aligned(chip, rows), rows), :]
        for slot, who in ((1, core), (2, 1 - core)):
            outs[slot][...] = y_ref[pl.ds(aligned(chip * 2 + who, block_rows), block_rows), :]
        for k in range(n):
            count = blocks[k].shape[0]
            product = dot(l_refs[k][...].reshape(count * rows, full), y_now)
            product = product.reshape(count, rows, columns)
            for p in range(count):
                term = product[p] * w[starts[k] + p].astype(F32)
                if not fresh:
                    term = term + p_refs[k][p]
                outs[3 + k][p] = term

    outs = [((rows, columns), F32), ((block_rows, columns), BF16), ((block_rows, columns), BF16)]
    outs += [((b.shape[0], rows, columns), F32) for b in blocks]
    arrays = [y, inverse] + list(blocks) + ([] if fresh else list(pendings))
    return call(body, outs, scalars, arrays, [pltpu.VMEM((full, columns), F32)], "push_rest")


def pull_level(scalars, level, gathered, crit, inverse, summed, chips, at):
    rows, columns = gathered[0].shape
    full = inverse.shape[0]
    n = len(gathered)
    n_sum = 0 if summed is None else 1

    def body(s, w, *refs):
        g_refs = refs[:n]
        crit_ref, inv_ref = refs[n : n + 2]
        sum_ref = refs[n + 2] if n_sum else None
        outs = refs[n + 2 + n_sum : -2]
        stack_ref, turned_ref = refs[-2:]
        chip, low, width = s[0], s[2] & (n - 1), s[3 + level]
        for k in range(n):
            p = low ^ k
            weighted = g_refs[k][...].astype(F32) * w[at + p].astype(F32)
            stack_ref[pl.ds(aligned(p, rows), rows), :] = weighted.astype(BF16)
        pulled = dot(stack_ref[...].T, crit_ref[...].reshape(n * rows, full))
        if n_sum:
            pulled = pulled + sum_ref[...]
        keep = lax.broadcasted_iota(jnp.int32, (columns, full), 1) < width
        pulled = jnp.where(keep, pulled, 0.0).astype(BF16)
        turned_ref[...] = jnp.where(keep, dot(pulled, inv_ref[...]), 0.0).T
        for k in range(chips):
            rows_out = turned_ref[pl.ds(aligned(chip ^ k, rows), rows), :]
            outs[k][...] = rows_out.astype(outs[k].dtype)

    outs = [((rows, columns), F32)] + [((rows, columns), BF16)] * (chips - 1)
    arrays = list(gathered) + [crit, inverse] + [summed] * n_sum
    scratch = [pltpu.VMEM((n * rows, columns), BF16), pltpu.VMEM((full, columns), F32)]
    return call(body, outs, scalars, arrays, scratch, "pull_level")


def pull_rest(scalars, gathered, blocks, sums, starts):
    rows, columns = gathered[0].shape
    full = blocks[0].shape[2]
    n, m = len(gathered), len(blocks)
    fresh = sums is None

    def body(s, w, *refs):
        g_refs = refs[:n]
        l_refs = refs[n : n + m]
        s_refs = refs[n + m : n + m + (0 if fresh else m)]
        outs, stack_ref = refs[n + m + (0 if fresh else m) : -1], refs[-1]
        low = s[2] & (n - 1)
        for k in range(m):
            for i in range(n):
                p = low ^ i
                weighted = g_refs[i][...].astype(F32) * w[starts[k] + p].astype(F32)
                stack_ref[pl.ds(aligned(p, rows), rows), :] = weighted.astype(BF16)
            term = dot(stack_ref[...].T, l_refs[k][...].reshape(n * rows, full))
            if not fresh:
                term = term + s_refs[k][...]
            outs[k][...] = term

    outs = [((columns, full), F32)] * m
    arrays = list(gathered) + list(blocks) + ([] if fresh else list(sums))
    scratch = [pltpu.VMEM((n * rows, columns), BF16)]
    return call(body, outs, scalars, arrays, scratch, "pull_rest")


def shards(rhs, diag_inverse, factor, widths, structure):
    leaf_count = lax.axis_size("leaf")
    chips = lax.axis_size("row") // 2
    leaf = lax.axis_index("leaf")
    row = lax.axis_index("row")
    chip, core = row // 2, row % 2
    levels, block_rows = rhs.shape[0], rhs.shape[2]
    rows = 2 * block_rows
    half = rhs.shape[3] // 2
    first = core == 0
    offsets = block_offsets(levels, leaf_count)

    def in_order(mine, theirs, axis):
        return jnp.where(
            first,
            jnp.concatenate([mine, theirs], axis),
            jnp.concatenate([theirs, mine], axis),
        )

    left_half, right_half = rhs[:, 0, :, :half], rhs[:, 0, :, half:]
    rhs_theirs = from_partner(jnp.where(first, right_half, left_half), "row", 1)
    rhs_pair = in_order(jnp.where(first, left_half, right_half), rhs_theirs, 1)
    places = jnp.stack([chip, core, leaf]).astype(jnp.int32)
    scalars = [jnp.concatenate([places, widths[:, 0]]), structure[0]]

    own_blocks = factor[0]
    their_blocks = from_partner(own_blocks, "row", 1)
    order = [(s, t) for s in range(levels) for t in range(s + 1, levels)]
    spans = [(offsets[pair], group_size(pair[1], leaf_count)) for pair in order]
    block = dict(
        zip(order, assemble(scalars[0], own_blocks, their_blocks, spans, block_rows))
    )

    def exchange_chips(pieces):
        return [from_partner(piece, "row", 2 * k) for k, piece in enumerate(pieces, 1)]

    def exchange_leaves(pieces):
        return [from_partner(piece, "leaf", k) for k, piece in enumerate(pieces, 1)]

    pending = {t: None for t in range(levels)}
    turned, kept, sent = [], [], []
    for l in range(levels):
        if l == 0:
            residual = rhs_pair[l]
        else:
            update = partial_own
            for piece in exchange_leaves(messages):
                update = update + piece.astype(F32)
            residual = (rhs_pair[l].astype(F32) - update).astype(BF16)
        parts = [residual] + exchange_chips([residual] * (chips - 1))
        inverse = diag_inverse[0, l]
        if l + 1 < levels:
            group = group_size(l + 1, leaf_count)
            y, partial_own, *messages = solve_and_push(
                scalars, l, parts, inverse, block[l, l + 1], pending[l + 1], group, offsets[l, l + 1]
            )
        else:
            (y,) = solve_and_push(scalars, l, parts, inverse, None, None, 1, 0)
        later = list(range(l + 2, levels))
        before = None if l == 0 else [pending[t] for t in later]
        starts = [offsets[l, t] for t in later]
        turned_now, keep, send, *after = push_rest(
            scalars, l, y, inverse, [block[l, t] for t in later], before, starts, block_rows, rows
        )
        pending.update(zip(later, after))
        turned.append(turned_now)
        kept.append(keep)
        sent.append(send)
    forward = in_order(jnp.stack(kept), from_partner(jnp.stack(sent), "row", 1), 2)

    sums = {l: None for l in range(levels)}
    adjoint = [None] * levels
    for l in reversed(range(levels)):
        value = turned[l]
        if l + 1 < levels:
            own_term, *messages = pull_level(
                scalars,
                l,
                gathered,
                block[l, l + 1],
                diag_inverse[0, l],
                sums[l],
                chips,
                offsets[l, l + 1],
            )
            total = own_term
            for piece in exchange_chips(messages):
                total = total + piece.astype(F32)
            value = value - total
        now = value.astype(BF16)
        adjoint[l] = now
        if l > 0:
            group = group_size(l, leaf_count)
            gathered = [now] + exchange_leaves([now] * (group - 1))
            sources = list(range(l - 1))
            if sources:
                before = None if l + 1 == levels else [sums[s] for s in sources]
                starts = [offsets[s, l] for s in sources]
                after = pull_rest(scalars, gathered, [block[s, l] for s in sources], before, starts)
                sums.update(zip(sources, after))
    stacked = jnp.stack(adjoint)
    low_rows, high_rows = stacked[:, :block_rows], stacked[:, block_rows:]
    theirs = from_partner(jnp.where(first, high_rows, low_rows), "row", 1)
    backward = in_order(jnp.where(first, low_rows, high_rows), theirs, 2)
    return forward[:, None], backward[:, None]


def solution(mesh):
    placed = (
        P(None, "leaf", "row", None),
        P("leaf", None, None, None),
        P("leaf", None, "row", None),
        P(None, "leaf"),
        P("leaf", None),
    )
    return jax.shard_map(
        shards,
        mesh=mesh,
        in_specs=placed,
        out_specs=(P(None, "leaf", "row", None), P(None, "leaf", "row", None)),
        check_vma=False,
    )
```

```python
import jax
import jax.numpy as jnp
from jax import lax
from jax.experimental import pallas as pl
from jax.experimental.pallas import tpu as pltpu
from jax.sharding import PartitionSpec as P


F32 = jnp.float32
BF16 = jnp.bfloat16
VMEM_LIMIT = 12 * 2**20


def chip_order(count):
    return tuple(sorted(range(1, count + 1), key=lambda k: (-k.bit_length(), k)))


def leaf_order(count):
    return tuple(range(count, 0, -1))


def from_partner(x, axis, mask):
    return lax.ppermute(x, axis, [(i, i ^ mask) for i in range(lax.axis_size(axis))])


def group_size(level_now, leaf_count):
    return min(2**level_now, leaf_count)


def block_offsets(levels, leaf_count):
    offset_table = {}
    cursor = 0
    for source_level in range(levels):
        for target_level in range(source_level + 1, levels):
            offset_table[source_level, target_level] = cursor
            cursor += group_size(target_level, leaf_count)
    return offset_table


def dot(left, right):
    return jnp.dot(left, right, preferred_element_type=F32)


def call(body, outs, scalars, arrays, scratch=(), limit=VMEM_LIMIT, anywhere=False):
    vmem = pl.BlockSpec(memory_space=pltpu.VMEM)
    given = pl.BlockSpec(memory_space=pltpu.HBM) if anywhere else vmem
    return pl.pallas_call(
        body,
        out_shape=[jax.ShapeDtypeStruct(s, d) for s, d in outs],
        in_specs=[pl.BlockSpec(memory_space=pltpu.SMEM)] * len(scalars) + [given] * len(arrays),
        out_specs=[vmem] * len(outs),
        scratch_shapes=list(scratch),
        compiler_params=pltpu.CompilerParams(vmem_limit_bytes=limit),
    )(*scalars, *arrays)


def aligned(index, size):
    return pl.multiple_of(index * size, size)


def assemble(scalars, own, theirs, places, block_rows):
    width = own.shape[2]
    n = len(places)

    def body(s, own_ref, their_ref, *refs):
        outs, sem = refs[:n], refs[n]
        core = s[1]
        copies = []
        for k, (at, count) in enumerate(places):
            for source, who in ((own_ref, core), (their_ref, 1 - core)):
                copies.append(
                    pltpu.make_async_copy(
                        source.at[pl.ds(at, count)],
                        outs[k].at[:, pl.ds(aligned(who, block_rows), block_rows), :],
                        sem.at[len(copies)],
                    )
                )
        for copy in copies:
            copy.start()
        for copy in copies:
            copy.wait()

    outs = [((count, 2 * block_rows, width), BF16) for _, count in places]
    scratch = [pltpu.SemaphoreType.DMA((2 * n,))]
    return call(body, outs, [scalars], [own, theirs], scratch, anywhere=True)


def solve_and_push(scalars, level, parts, inverse, crit, pending, group, at):
    rows, columns = parts[0].shape
    full = inverse.shape[0]
    n_parts, n_pend = len(parts), 0 if pending is None else 1
    n_crit = 0 if crit is None else 1

    def body(s, w, *refs):
        part_refs = refs[:n_parts]
        inv_ref = refs[n_parts]
        crit_ref = refs[n_parts + 1] if n_crit else None
        pend_ref = refs[n_parts + 2] if n_pend else None
        out = n_parts + 1 + n_crit + n_pend
        y_ref = refs[out]
        outs, x_ref = refs[out + 1 : -1], refs[-1]
        chip, low, width = s[0], s[2] & (group - 1), s[3 + level]
        for k in range(n_parts):
            x_ref[pl.ds(aligned(chip ^ k, rows), rows), :] = part_refs[k][...]
        keep = lax.broadcasted_iota(jnp.int32, (full, columns), 0) < width
        x = jnp.where(keep, x_ref[...], jnp.zeros((), BF16))
        y = jnp.where(keep, dot(inv_ref[...], x), 0.0).astype(BF16)
        y_ref[...] = y
        for k in range(len(outs)):
            p = low ^ k
            product = dot(crit_ref[p], y) * w[at + p].astype(F32)
            if n_pend:
                product = product + pend_ref[p]
            outs[k][...] = product.astype(outs[k].dtype)

    outs = [((full, columns), BF16)]
    if n_crit:
        outs.append(((rows, columns), F32))
        outs += [((rows, columns), BF16)] * (group - 1)
    arrays = list(parts) + [inverse] + [crit] * n_crit + [pending] * n_pend
    return call(body, outs, scalars, arrays, [pltpu.VMEM((full, columns), BF16)])


def push_rest(scalars, level, y, inverse, blocks, pendings, starts, block_rows, rows):
    full, columns = y.shape
    n = len(blocks)
    fresh = pendings is None

    def body(s, w, *refs):
        y_ref, inv_ref = refs[:2]
        l_refs = refs[2 : 2 + n]
        p_refs = refs[2 + n : 2 + n + (0 if fresh else n)]
        outs = refs[2 + n + (0 if fresh else n) : -1]
        turned_ref = refs[-1]
        chip, core, width = s[0], s[1], s[3 + level]
        y_now = y_ref[...]
        keep = lax.broadcasted_iota(jnp.int32, (full, columns), 0) < width
        turned_ref[...] = jnp.where(keep, dot(y_now.T, inv_ref[...]).T, 0.0)
        outs[0][...] = turned_ref[pl.ds(aligned(chip, rows), rows), :]
        for slot, who in ((1, core), (2, 1 - core)):
            outs[slot][...] = y_ref[pl.ds(aligned(chip * 2 + who, block_rows), block_rows), :]
        for k in range(n):
            count = blocks[k].shape[0]
            product = dot(l_refs[k][...].reshape(count * rows, full), y_now)
            product = product.reshape(count, rows, columns)
            for p in range(count):
                term = product[p] * w[starts[k] + p].astype(F32)
                if not fresh:
                    term = term + p_refs[k][p]
                outs[3 + k][p] = term

    outs = [((rows, columns), F32), ((block_rows, columns), BF16), ((block_rows, columns), BF16)]
    outs += [((b.shape[0], rows, columns), F32) for b in blocks]
    arrays = [y, inverse] + list(blocks) + ([] if fresh else list(pendings))
    return call(body, outs, scalars, arrays, [pltpu.VMEM((full, columns), F32)])


def pull_level(scalars, level, gathered, crit, inverse, summed, chips, at):
    rows, columns = gathered[0].shape
    full = inverse.shape[0]
    n = len(gathered)
    n_sum = 0 if summed is None else 1

    def body(s, w, *refs):
        g_refs = refs[:n]
        crit_ref, inv_ref = refs[n : n + 2]
        sum_ref = refs[n + 2] if n_sum else None
        outs = refs[n + 2 + n_sum : -2]
        stack_ref, turned_ref = refs[-2:]
        chip, low, width = s[0], s[2] & (n - 1), s[3 + level]
        for k in range(n):
            p = low ^ k
            weighted = g_refs[k][...].astype(F32) * w[at + p].astype(F32)
            stack_ref[pl.ds(aligned(p, rows), rows), :] = weighted.astype(BF16)
        pulled = dot(stack_ref[...].T, crit_ref[...].reshape(n * rows, full))
        if n_sum:
            pulled = pulled + sum_ref[...]
        keep = lax.broadcasted_iota(jnp.int32, (columns, full), 1) < width
        pulled = jnp.where(keep, pulled, 0.0).astype(BF16)
        turned_ref[...] = jnp.where(keep, dot(pulled, inv_ref[...]), 0.0).T
        for k in range(chips):
            rows_out = turned_ref[pl.ds(aligned(chip ^ k, rows), rows), :]
            outs[k][...] = rows_out.astype(outs[k].dtype)

    outs = [((rows, columns), F32)] + [((rows, columns), BF16)] * (chips - 1)
    arrays = list(gathered) + [crit, inverse] + [summed] * n_sum
    scratch = [pltpu.VMEM((n * rows, columns), BF16), pltpu.VMEM((full, columns), F32)]
    return call(body, outs, scalars, arrays, scratch)


def pull_rest(scalars, gathered, blocks, sums, starts):
    rows, columns = gathered[0].shape
    full = blocks[0].shape[2]
    n, m = len(gathered), len(blocks)
    fresh = sums is None

    def body(s, w, *refs):
        g_refs = refs[:n]
        l_refs = refs[n : n + m]
        s_refs = refs[n + m : n + m + (0 if fresh else m)]
        outs, stack_ref = refs[n + m + (0 if fresh else m) : -1], refs[-1]
        low = s[2] & (n - 1)
        for k in range(m):
            for i in range(n):
                p = low ^ i
                weighted = g_refs[i][...].astype(F32) * w[starts[k] + p].astype(F32)
                stack_ref[pl.ds(aligned(p, rows), rows), :] = weighted.astype(BF16)
            term = dot(stack_ref[...].T, l_refs[k][...].reshape(n * rows, full))
            if not fresh:
                term = term + s_refs[k][...]
            outs[k][...] = term

    outs = [((columns, full), F32)] * m
    arrays = list(gathered) + list(blocks) + ([] if fresh else list(sums))
    scratch = [pltpu.VMEM((n * rows, columns), BF16)]
    return call(body, outs, scalars, arrays, scratch)


def shards(rhs, diag_inverse, factor, widths, structure):
    leaf_count = lax.axis_size("leaf")
    chips = lax.axis_size("row") // 2
    leaf = lax.axis_index("leaf")
    row = lax.axis_index("row")
    chip, core = row // 2, row % 2
    levels, block_rows = rhs.shape[0], rhs.shape[2]
    rows = 2 * block_rows
    half = rhs.shape[3] // 2
    first = core == 0
    offsets = block_offsets(levels, leaf_count)

    def in_order(mine, theirs, axis):
        return jnp.where(
            first,
            jnp.concatenate([mine, theirs], axis),
            jnp.concatenate([theirs, mine], axis),
        )

    left_half, right_half = rhs[:, 0, :, :half], rhs[:, 0, :, half:]
    rhs_theirs = from_partner(jnp.where(first, right_half, left_half), "row", 1)
    rhs_pair = in_order(jnp.where(first, left_half, right_half), rhs_theirs, 1)
    places = jnp.stack([chip, core, leaf]).astype(jnp.int32)
    scalars = [jnp.concatenate([places, widths[:, 0]]), structure[0]]

    own_blocks = factor[0]
    their_blocks = from_partner(own_blocks, "row", 1)
    order = [(s, t) for s in range(levels) for t in range(s + 1, levels)]
    spans = [(offsets[pair], group_size(pair[1], leaf_count)) for pair in order]
    block = dict(
        zip(order, assemble(scalars[0], own_blocks, their_blocks, spans, block_rows))
    )

    def exchange(pieces, axis, scale, order):
        taken = {}
        for k in order:
            taken[k] = from_partner(pieces[k - 1], axis, scale * k)
        return [taken[k] for k in sorted(taken)]

    def exchange_chips(pieces):
        return exchange(pieces, "row", 2, chip_order(len(pieces)))

    def exchange_leaves(pieces):
        return exchange(pieces, "leaf", 1, leaf_order(len(pieces)))

    pending = {t: None for t in range(levels)}
    turned, kept, sent = [], [], []
    for l in range(levels):
        if l == 0:
            residual = rhs_pair[l]
        else:
            update = partial_own
            for piece in exchange_leaves(messages):
                update = update + piece.astype(F32)
            residual = (rhs_pair[l].astype(F32) - update).astype(BF16)
        parts = [residual] + exchange_chips([residual] * (chips - 1))
        inverse = diag_inverse[0, l]
        if l + 1 < levels:
            group = group_size(l + 1, leaf_count)
            y, partial_own, *messages = solve_and_push(
                scalars, l, parts, inverse, block[l, l + 1], pending[l + 1], group, offsets[l, l + 1]
            )
        else:
            (y,) = solve_and_push(scalars, l, parts, inverse, None, None, 1, 0)
        later = list(range(l + 2, levels))
        before = None if l == 0 else [pending[t] for t in later]
        starts = [offsets[l, t] for t in later]
        turned_now, keep, send, *after = push_rest(
            scalars, l, y, inverse, [block[l, t] for t in later], before, starts, block_rows, rows
        )
        pending.update(zip(later, after))
        turned.append(turned_now)
        kept.append(keep)
        sent.append(send)
    forward = in_order(jnp.stack(kept), from_partner(jnp.stack(sent), "row", 1), 2)

    sums = {l: None for l in range(levels)}
    adjoint = [None] * levels
    for l in reversed(range(levels)):
        value = turned[l]
        if l + 1 < levels:
            own_term, *messages = pull_level(
                scalars,
                l,
                gathered,
                block[l, l + 1],
                diag_inverse[0, l],
                sums[l],
                chips,
                offsets[l, l + 1],
            )
            total = own_term
            for piece in exchange_chips(messages):
                total = total + piece.astype(F32)
            value = value - total
        now = value.astype(BF16)
        adjoint[l] = now
        if l > 0:
            group = group_size(l, leaf_count)
            gathered = [now] + exchange_leaves([now] * (group - 1))
            sources = list(range(l - 1))
            if sources:
                before = None if l + 1 == levels else [sums[s] for s in sources]
                starts = [offsets[s, l] for s in sources]
                after = pull_rest(scalars, gathered, [block[s, l] for s in sources], before, starts)
                sums.update(zip(sources, after))
    stacked = jnp.stack(adjoint)
    low_rows, high_rows = stacked[:, :block_rows], stacked[:, block_rows:]
    theirs = from_partner(jnp.where(first, high_rows, low_rows), "row", 1)
    backward = in_order(jnp.where(first, low_rows, high_rows), theirs, 2)
    return forward[:, None], backward[:, None]


def solution(mesh):
    placed = (
        P(None, "leaf", "row", None),
        P("leaf", None, None, None),
        P("leaf", None, "row", None),
        P(None, "leaf"),
        P("leaf", None),
    )

    def solve(rhs, diag_inverse, factor, widths, structure):
        step = jax.shard_map(
            shards,
            mesh=mesh,
            in_specs=placed,
            out_specs=(P(None, "leaf", "row", None), P(None, "leaf", "row", None)),
            check_vma=False,
        )
        return step(rhs, diag_inverse, factor, widths, structure)

    return solve
```

```python
import jax
import jax.numpy as jnp
from jax import lax
from jax.experimental import pallas as pl
from jax.experimental.pallas import tpu as pltpu
from jax.sharding import PartitionSpec as P


F32 = jnp.float32
BF16 = jnp.bfloat16
VMEM_LIMIT = 16 * 2**20
SKIP_LEVEL = 4


def chip_order(count):
    return tuple(sorted(range(1, count + 1), key=lambda k: (-k.bit_length(), k)))


def leaf_order(count):
    return tuple(range(count, 0, -1))


def from_partner(x, axis, mask):
    return lax.ppermute(x, axis, [(i, i ^ mask) for i in range(lax.axis_size(axis))])


def group_size(level_now, leaf_count):
    return min(2**level_now, leaf_count)


def block_offsets(levels, leaf_count):
    offset_table = {}
    cursor = 0
    for source_level in range(levels):
        for target_level in range(source_level + 1, levels):
            offset_table[source_level, target_level] = cursor
            cursor += group_size(target_level, leaf_count)
    return offset_table


def dot(left, right):
    return jnp.dot(left, right, preferred_element_type=F32)


def call(body, outs, scalars, arrays, scratch=(), far=0):
    vmem = pl.BlockSpec(memory_space=pltpu.VMEM)
    given = [pl.BlockSpec(memory_space=pltpu.HBM)] * far + [vmem] * (len(arrays) - far)
    return pl.pallas_call(
        body,
        out_shape=[jax.ShapeDtypeStruct(s, d) for s, d in outs],
        in_specs=[pl.BlockSpec(memory_space=pltpu.SMEM)] * len(scalars) + given,
        out_specs=[vmem] * len(outs),
        scratch_shapes=list(scratch),
        compiler_params=pltpu.CompilerParams(vmem_limit_bytes=VMEM_LIMIT),
    )(*scalars, *arrays)


def aligned(index, size):
    return pl.multiple_of(index * size, size)


def masked_inverse(inverse, width):
    full = inverse.shape[0]
    down = lax.broadcasted_iota(jnp.int32, (full, full), 0) < width
    along = lax.broadcasted_iota(jnp.int32, (full, full), 1) < width
    return jnp.where(down & along, inverse, jnp.zeros((), BF16))


def fold_blocks(scalars, factor, inverses, spans, picked, blocks, levels, keep):
    _, half, full = factor.shape
    total = sum(count for _, _, count in spans)
    n_out = 1 + len(picked)

    def body(s, w, factor_ref, inverses_ref, *refs):
        out_ref, picked_refs = refs[0], refs[1:n_out]
        own_ref, inv_ref, folded_ref, sem = refs[n_out:]
        used = sorted({level for level, _, _ in spans})
        order = used + [level for level in range(levels) if level not in used]
        copies = [pltpu.make_async_copy(factor_ref.at[pl.ds(0, blocks)], own_ref, sem.at[levels])]
        copies += [
            pltpu.make_async_copy(inverses_ref.at[level], inv_ref.at[level], sem.at[level])
            for level in order
        ]
        for copy in copies:
            copy.start()
        copies.pop(0).wait()
        cursor, last = 0, None
        for i, (level, at, count) in enumerate(spans):
            if level != last:
                copies.pop(0).wait()
                folded_ref[used.index(level)] = masked_inverse(inv_ref[level], s[3 + level])
                last = level
            flat = own_ref[pl.ds(at, count)].reshape(count * half, full)
            product = dot(flat, folded_ref[used.index(level)]).reshape(count, half, full)
            for p in range(count):
                block = (product[p] * w[at + p].astype(F32)).astype(BF16)
                out_ref[cursor + p] = block
                if i in picked:
                    picked_refs[picked.index(i)][p] = block
            cursor += count
        for copy in copies:
            copy.wait()

    outs = [((total, half, full), BF16)]
    outs += [((spans[i][2], half, full), BF16) for i in picked]
    held = [((blocks, half, full), BF16), ((levels, full, full), BF16)]
    scratch = [] if keep else [pltpu.VMEM(*h) for h in held]
    n_used = len({level for level, _, _ in spans})
    scratch += [pltpu.VMEM((n_used, full, full), BF16), pltpu.SemaphoreType.DMA((levels + 1,))]
    arrays = [pltpu.with_memory_space_constraint(x, pltpu.HBM) for x in (factor, inverses)]
    return call(body, outs + (held if keep else []), scalars, arrays, scratch, far=2)


def skip_level(scalars, upper, lower_mine, lower_theirs, folded, at):
    count, half, full = upper[0].shape
    n, chips = len(upper), len(lower_mine)

    def body(s, *refs):
        upper_refs, mine = refs[:n], refs[n : n + chips]
        theirs, folded_ref, out_ref, lower_ref = refs[n + chips :]
        chip, core, leaf = s[0], s[1], s[2]
        total = jnp.zeros((count * half, full), F32)
        for k in range(n):
            p = (leaf ^ k) & (n - 1)
            for q in range(chips):
                place = (chip ^ q) * 2
                lower_ref[k, pl.ds(aligned(place + core, half), half), :] = mine[q][p]
                lower_ref[k, pl.ds(aligned(place + 1 - core, half), half), :] = theirs[q, p]
            total = total + dot(upper_refs[k][...].reshape(count * half, full), lower_ref[k])
        direct = folded_ref[pl.ds(at, count)].astype(F32)
        out_ref[...] = (direct - total.reshape(count, half, full)).astype(BF16)

    outs = [((count, half, full), BF16)]
    arrays = [*upper, *lower_mine, lower_theirs, folded]
    return call(body, outs, scalars[:1], arrays, [pltpu.VMEM((n, full, full), BF16)])


def push(scalars, parts, full, group, pending, pair, at):
    rows, columns = parts[0].shape
    half = rows // 2
    n_parts = len(parts)
    n_pend = 0 if pending is None else 1

    def body(s, *refs):
        part_refs, m_refs = refs[:n_parts], refs[n_parts : n_parts + 2]
        pend_ref = refs[n_parts + 2] if n_pend else None
        outs, x_ref, all_ref = refs[n_parts + 2 + n_pend : -2], *refs[-2:]
        chip, core, leaf = s[0], s[1], s[2]
        for k in range(n_parts):
            x_ref[pl.ds(aligned(chip ^ k, rows), rows), :] = part_refs[k][...]
        for side in range(2):
            flat = m_refs[side][pl.ds(at, group)].reshape(group * half, full)
            all_ref[side] = dot(flat, x_ref[...]).reshape(group, half, columns)
        for k in range(group):
            p = (leaf ^ k) & (group - 1)
            for side, who in enumerate((core, 1 - core)):
                place = pl.ds(aligned(who, half), half)
                total = all_ref[side, p]
                if n_pend:
                    total = total + pend_ref[p, place, :]
                outs[k][place, :] = total.astype(outs[k].dtype)

    outs = [((rows, columns), BF16 if k else F32) for k in range(group)]
    arrays = [*parts, *pair, *([pending] if n_pend else [])]
    scratch = [
        pltpu.VMEM((full, columns), BF16),
        pltpu.VMEM((2, group, half, columns), F32),
    ]
    return call(body, outs, scalars[:1], arrays, scratch)


def finish(scalars, level, parts, inverses, sides, spans, pendings):
    rows, columns = parts[0].shape
    full = inverses.shape[1]
    half = rows // 2
    n, n_parts = len(spans), len(parts)
    n_s = 2 if n else 0
    fresh = pendings is None

    def body(s, w, *refs):
        part_refs, inv_ref = refs[:n_parts], refs[n_parts]
        refs = refs[n_parts + 1 :]
        side_refs, p_refs = refs[:n_s], refs[n_s : n_s + (0 if fresh else n)]
        outs, x_ref, turned_ref, y_ref = refs[n_s + (0 if fresh else n) : -3], *refs[-3:]
        chip, core, width = s[0], s[1], s[3 + level]
        for k in range(n_parts):
            x_ref[pl.ds(aligned(chip ^ k, rows), rows), :] = part_refs[k][...]
        keep = lax.broadcasted_iota(jnp.int32, (full, columns), 0) < width
        x = jnp.where(keep, x_ref[...], jnp.zeros((), BF16))
        y = jnp.where(keep, dot(inv_ref[level], x), 0.0).astype(BF16)
        y_ref[...] = y
        turned_ref[...] = jnp.where(keep, dot(y.T, inv_ref[level]).T, 0.0)
        outs[0][...] = turned_ref[pl.ds(aligned(chip, rows), rows), :]
        for at, who in ((1, core), (2, 1 - core)):
            outs[at][...] = y_ref[pl.ds(aligned(chip * 2 + who, half), half), :]
        for k, (at, count) in enumerate(spans):
            for side, who in enumerate((core, 1 - core)):
                place = pl.ds(aligned(who, half), half)
                product = dot(side_refs[side][pl.ds(at, count)].reshape(count * half, full), y)
                product = product.reshape(count, half, columns)
                for p in range(count):
                    term = product[p] * w[at + p].astype(F32)
                    if not fresh:
                        term = term + p_refs[k][p, place, :]
                    outs[3 + k][p, place, :] = term

    outs = [((rows, columns), F32), ((half, columns), BF16), ((half, columns), BF16)]
    outs += [((count, rows, columns), F32) for _, count in spans]
    arrays = [*parts, inverses, *(sides if n else []), *([] if fresh else pendings)]
    scratch = [
        pltpu.VMEM((full, columns), BF16),
        pltpu.VMEM((full, columns), F32),
        pltpu.VMEM((full, columns), BF16),
    ]
    return call(body, outs, scalars, arrays, scratch)


def two_sides(stack_ref, piece_refs, vector, leaf, core, weights=None):
    count = len(vector)
    half = piece_refs[0].shape[1] // 2
    for k, (array, slot) in enumerate(vector):
        p = (leaf ^ k) & (count - 1)
        for side, who in enumerate((core, 1 - core)):
            piece = piece_refs[array][slot, pl.ds(aligned(who, half), half), :]
            if weights is not None:
                w, start = weights
                piece = (piece.astype(F32) * w[start + p].astype(F32)).astype(BF16)
            stack_ref[side, pl.ds(aligned(p, half), half), :] = piece
    return [stack_ref[side, : count * half, :].T for side in range(2)]


def pull(scalars, pieces, vectors, outputs, pairs, full, chips):
    _, rows, columns = pieces[0].shape
    half = rows // 2
    n_p, n_m = len(pieces), 2 * len(pairs)
    sums = [total for _, total in outputs if total is not None]
    tall = max(len(v) for v in vectors) * half

    def body(s, *refs):
        piece_refs, m_refs = refs[:n_p], refs[n_p : n_p + n_m]
        waiting = list(refs[n_p + n_m : n_p + n_m + len(sums)])
        outs, stack_ref, turned_ref = refs[n_p + n_m + len(sums) : -2], *refs[-2:]
        chip, core, leaf = s[0], s[1], s[2]
        lefts = [
            two_sides(stack_ref.at[i], piece_refs, v, leaf, core) for i, v in enumerate(vectors)
        ]
        for slot, (terms, total) in enumerate(outputs):
            now = None if total is None else waiting.pop(0)[...]
            for v, which, at in terms:
                count = len(vectors[v])
                for side in range(2):
                    flat = m_refs[2 * which + side][pl.ds(at, count)].reshape(count * half, full)
                    product = dot(lefts[v][side], flat)
                    now = product if now is None else now + product
            turned_ref[slot] = now.T
            for k in range(chips):
                block = turned_ref[slot, pl.ds(aligned(chip ^ k, rows), rows), :]
                outs[k][slot] = block.astype(outs[k].dtype)

    outs = [((len(outputs), rows, columns), BF16 if k else F32) for k in range(chips)]
    arrays = [*pieces, *[m for pair in pairs for m in pair], *sums]
    scratch = [
        pltpu.VMEM((len(vectors), 2, tall, columns), BF16),
        pltpu.VMEM((len(outputs), full, columns), F32),
    ]
    return call(body, outs, scalars[:1], arrays, scratch)


def pull_rest(scalars, pieces, vectors, outputs, sides, inverses):
    _, rows, columns = pieces[0].shape
    half = rows // 2
    full = inverses.shape[1]
    n_p = len(pieces)
    sums = [o[2] for o in outputs if o[2] is not None]
    tall = max(len(v) for v in vectors) * half

    def body(s, w, *refs):
        piece_refs, side_refs, inv_ref = refs[:n_p], refs[n_p : n_p + 2], refs[n_p + 2]
        waiting = list(refs[n_p + 3 : n_p + 3 + len(sums)])
        outs, stack_ref = refs[n_p + 3 + len(sums) : -1], refs[-1]
        core, leaf = s[1], s[2]
        for slot, (level, terms, total, complete) in enumerate(outputs):
            now = None if total is None else waiting.pop(0)[...]
            for v, at in terms:
                count = len(vectors[v])
                lefts = two_sides(
                    stack_ref.at[slot], piece_refs, vectors[v], leaf, core, (w, at)
                )
                for side in range(2):
                    flat = side_refs[side][pl.ds(at, count)].reshape(count * half, full)
                    product = dot(lefts[side], flat)
                    now = product if now is None else now + product
            if complete:
                keep = lax.broadcasted_iota(jnp.int32, (columns, full), 1) < s[3 + level]
                now = jnp.where(keep, now, 0.0).astype(BF16)
                now = jnp.where(keep, dot(now, inv_ref[level]), 0.0)
            outs[slot][...] = now

    outs = [((columns, full), F32)] * len(outputs)
    arrays = [*pieces, *sides, inverses, *sums]
    return call(body, outs, scalars, arrays, [pltpu.VMEM((len(outputs), 2, tall, columns), BF16)])


def shards(rhs, diag_inverse, factor, widths, structure):
    leaf_count = lax.axis_size("leaf")
    chips = lax.axis_size("row") // 2
    leaf = lax.axis_index("leaf")
    row = lax.axis_index("row")
    chip, core = row // 2, row % 2
    levels, block_rows = rhs.shape[0], rhs.shape[2]
    half, full = rhs.shape[3] // 2, factor.shape[3]
    first = core == 0
    offsets = block_offsets(levels, leaf_count)
    group = [group_size(l, leaf_count) for l in range(levels)]
    top = levels - 1

    def in_order(mine, theirs, axis):
        return jnp.where(
            first,
            jnp.concatenate([mine, theirs], axis),
            jnp.concatenate([theirs, mine], axis),
        )

    def exchange(pieces, axis, scale, order):
        taken = {}
        for k in order:
            taken[k] = from_partner(pieces[k - 1], axis, scale * k)
        return [taken[k] for k in sorted(taken)]

    def exchange_chips(pieces):
        return exchange(pieces, "row", 2, chip_order(len(pieces)))

    def exchange_leaves(pieces):
        return exchange(pieces, "leaf", 1, leaf_order(len(pieces)))

    def gather_chips(stacked):
        return [stacked] + exchange_chips([stacked] * (chips - 1))

    left_half, right_half = rhs[:, 0, :, :half], rhs[:, 0, :, half:]
    rhs_theirs = from_partner(jnp.where(first, right_half, left_half), "row", 1)
    rhs_pair = in_order(jnp.where(first, left_half, right_half), rhs_theirs, 1)
    places = jnp.stack([chip, core, leaf]).astype(jnp.int32)
    scalars = [jnp.concatenate([places, widths[:, 0]]), structure[0]]

    folded_at = {}

    def fold(pairs, picked, blocks, levels, keep):
        cursor, spans = 0, []
        for s, t in pairs:
            folded_at[s, t] = cursor
            spans.append((s, offsets[s, t], group[t]))
            cursor += group[t]
        mine, half, *held = fold_blocks(
            scalars,
            factor[0],
            diag_inverse[0],
            spans,
            [pairs.index(picked)],
            blocks,
            levels,
            keep,
        )
        theirs = from_partner(mine, "row", 1)
        return (mine, theirs), half, held

    lowest = [(0, 1), (0, 2)]
    folded_first, lower_half, _ = fold(lowest, (0, 1), group[1] + group[2], 1, False)
    others = sorted([(s, s + 1) for s in range(1, top)] + [(1, 3)])
    folded, upper_half, (own_blocks, inverses) = fold(others, (1, 2), factor.shape[1], levels, True)
    their_blocks = from_partner(factor[0], "row", 1)
    sides = [own_blocks, their_blocks]
    lower_mine = gather_chips(lower_half)
    upper = [upper_half] + exchange_leaves([upper_half] * (group[1] - 1))

    def skip_product(lower_mine, upper, after):
        lower_mine, upper, _ = lax.optimization_barrier((lower_mine, upper, after))
        lower_theirs = from_partner(jnp.stack(lower_mine), "row", 1)
        (mine,) = skip_level(scalars, upper, lower_mine, lower_theirs, folded_first[0], folded_at[0, 2])
        theirs = from_partner(mine, "row", 1)
        return mine, theirs

    pending = {t: None for t in range(levels)}
    turned, kept, sent = [None] * levels, [None] * levels, [None] * levels

    def finish_level(l, parts):
        later = list(range(l + 2, levels))
        before = None if l == 0 else [pending[t] for t in later]
        spans = [(offsets[l, t], group[t]) for t in later]
        turned[l], kept[l], sent[l], *after = finish(
            scalars, l, parts, inverses, sides, spans, before
        )
        pending.update(zip(later, after))

    def push_level(l, parts):
        pair, at = folded if l else folded_first, folded_at[l, l + 1]
        return push(scalars, parts, full, group[l + 1], pending[l + 1], pair, at)

    parts = gather_chips(rhs_pair[0])
    own, *messages = push_level(0, parts)
    for l in range(1, levels):
        received = exchange_leaves(messages)
        finish_level(l - 1, parts)
        update = own
        for piece in received:
            update = update + piece.astype(F32)
        now = (rhs_pair[l].astype(F32) - update).astype(BF16)
        parts = gather_chips(now)
        if l < top:
            own, *messages = push_level(l, parts)
        if l == SKIP_LEVEL:
            skip = skip_product(lower_mine, upper, own)
    finish_level(top, parts)

    adjoint = [None] * levels

    def gather_leaves(named):
        span = max(group[l] for l, _ in named)
        listed = [[i for i, (l, _) in enumerate(named) if group[l] > k] for k in range(span)]
        stacks = [jnp.stack([named[i][1] for i in row]) for row in listed]
        pieces = [stacks[0]] + exchange_leaves(stacks[1:])
        vectors = [
            [(k, listed[k].index(i)) for k in range(group[l])] for i, (l, _) in enumerate(named)
        ]
        return pieces, vectors

    def total_of(own, received, slot):
        total = own[slot]
        for piece in received:
            total = total + piece[slot].astype(F32)
        return total

    adjoint[top] = turned[top].astype(BF16)
    pieces, vectors = gather_leaves([(top, adjoint[top])])
    sums = {s: None for s in range(levels)}
    for l in range(top - 1, 1, -1):
        t = l + 1
        outputs = [([(0, 0, folded_at[l, t])], sums[l])]
        if l == 2:
            outputs.append(([(0, 0, folded_at[1, t])], sums[1]))
        own, *messages = pull(scalars, pieces, vectors, outputs, [folded], full, chips)
        received = exchange_chips(messages)
        sources = [s for s in range(t - 1) if (s, t) != (1, 3)]
        complete = {t - 2} if t > 4 else {1, 2} if t == 4 else {0}
        listed = [(s, [(0, offsets[s, t])], sums[s], s in complete) for s in sources]
        sums.update(zip(sources, pull_rest(scalars, pieces, vectors, listed, sides, inverses)))
        adjoint[l] = (turned[l] - total_of(own, received, 0)).astype(BF16)
        named = [(l, adjoint[l])]
        if l == 2:
            ahead = turned[1] - total_of(own, received, 1)
            named.append((1, ahead.astype(BF16)))
        pieces, vectors = gather_leaves(named)
    outputs = [
        ([(0, 1, 0), (1, 2, folded_at[0, 1])], sums[0]),
        ([(0, 0, folded_at[1, 2])], None),
    ]
    own, *messages = pull(scalars, pieces, vectors, outputs, [folded, skip, folded_first], full, chips)
    received = exchange_chips(messages)
    adjoint[0] = (turned[0] - total_of(own, received, 0)).astype(BF16)
    adjoint[1] = (ahead - total_of(own, received, 1)).astype(BF16)

    theirs = from_partner(jnp.stack(sent), "row", 1)
    forward = in_order(jnp.stack(kept), theirs, 2)

    def swap_rows(values):
        stacked = jnp.stack(values)
        low_rows, high_rows = stacked[:, :block_rows], stacked[:, block_rows:]
        theirs = from_partner(jnp.where(first, high_rows, low_rows), "row", 1)
        return in_order(jnp.where(first, low_rows, high_rows), theirs, 2)

    upper_levels = swap_rows(adjoint[2:])
    backward = jnp.concatenate([swap_rows(adjoint[:2]), upper_levels])
    return forward[:, None], backward[:, None]


def solution(mesh):
    placed = (
        P(None, "leaf", "row", None),
        P("leaf", None, None, None),
        P("leaf", None, "row", None),
        P(None, "leaf"),
        P("leaf", None),
    )

    def solve(rhs, diag_inverse, factor, widths, structure):
        step = jax.shard_map(
            shards,
            mesh=mesh,
            in_specs=placed,
            out_specs=(P(None, "leaf", "row", None), P(None, "leaf", "row", None)),
            check_vma=False,
        )
        return step(
            rhs, diag_inverse, factor, widths, structure
        )

    return solve
```

```python
import jax
import jax.numpy as jnp
from jax import lax
from jax.experimental import pallas as pl
from jax.experimental.pallas import tpu as pltpu
from jax.sharding import PartitionSpec as P


F32 = jnp.float32
BF16 = jnp.bfloat16
VMEM_LIMIT = 16 * 2**20
CUTS = 2


def chip_order(count):
    return tuple(sorted(range(1, count + 1), key=lambda k: (-k.bit_length(), k)))


def leaf_order(count):
    return tuple(range(count, 0, -1))


def from_partner(x, axis, mask):
    return lax.ppermute(x, axis, [(i, i ^ mask) for i in range(lax.axis_size(axis))])


def group_size(level_now, leaf_count):
    return min(2**level_now, leaf_count)


def block_offsets(levels, leaf_count):
    offset_table = {}
    cursor = 0
    for source_level in range(levels):
        for target_level in range(source_level + 1, levels):
            offset_table[source_level, target_level] = cursor
            cursor += group_size(target_level, leaf_count)
    return offset_table


def dot(left, right):
    return jnp.dot(left, right, preferred_element_type=F32)


def call(body, outs, scalars, arrays, scratch=(), far=0):
    vmem = pl.BlockSpec(memory_space=pltpu.VMEM)
    given = [pl.BlockSpec(memory_space=pltpu.HBM)] * far + [vmem] * (len(arrays) - far)
    return pl.pallas_call(
        body,
        out_shape=[jax.ShapeDtypeStruct(s, d) for s, d in outs],
        in_specs=[pl.BlockSpec(memory_space=pltpu.SMEM)] * len(scalars) + given,
        out_specs=[vmem] * len(outs),
        scratch_shapes=list(scratch),
        compiler_params=pltpu.CompilerParams(vmem_limit_bytes=VMEM_LIMIT),
    )(*scalars, *arrays)


def aligned(index, size):
    return pl.multiple_of(index * size, size)


def masked_inverse(inverse, width):
    full = inverse.shape[0]
    down = lax.broadcasted_iota(jnp.int32, (full, full), 0) < width
    along = lax.broadcasted_iota(jnp.int32, (full, full), 1) < width
    return jnp.where(down & along, inverse, jnp.zeros((), BF16))


def fold_blocks(scalars, factor, inverses, spans, picked, blocks, levels, keep):
    _, half, full = factor.shape
    total = sum(count for _, _, count in spans)
    n_out = 1 + len(picked)

    def body(s, w, factor_ref, inverses_ref, *refs):
        out_ref, picked_refs = refs[0], refs[1:n_out]
        own_ref, inv_ref, folded_ref, sem = refs[n_out:]
        used = sorted({level for level, _, _ in spans})
        order = used + [level for level in range(levels) if level not in used]
        copies = [pltpu.make_async_copy(factor_ref.at[pl.ds(0, blocks)], own_ref, sem.at[levels])]
        copies += [
            pltpu.make_async_copy(inverses_ref.at[level], inv_ref.at[level], sem.at[level])
            for level in order
        ]
        for copy in copies:
            copy.start()
        copies.pop(0).wait()
        cursor, last = 0, None
        for i, (level, at, count) in enumerate(spans):
            if level != last:
                copies.pop(0).wait()
                folded_ref[used.index(level)] = masked_inverse(inv_ref[level], s[3 + level])
                last = level
            flat = own_ref[pl.ds(at, count)].reshape(count * half, full)
            product = dot(flat, folded_ref[used.index(level)]).reshape(count, half, full)
            for p in range(count):
                block = (product[p] * w[at + p].astype(F32)).astype(BF16)
                out_ref[cursor + p] = block
                if i in picked:
                    picked_refs[picked.index(i)][p] = block
            cursor += count
        for copy in copies:
            copy.wait()

    outs = [((total, half, full), BF16)]
    outs += [((spans[i][2], half, full), BF16) for i in picked]
    held = [((blocks, half, full), BF16), ((levels, full, full), BF16)]
    scratch = [] if keep else [pltpu.VMEM(*h) for h in held]
    n_used = len({level for level, _, _ in spans})
    scratch += [pltpu.VMEM((n_used, full, full), BF16), pltpu.SemaphoreType.DMA((levels + 1,))]
    arrays = [pltpu.with_memory_space_constraint(x, pltpu.HBM) for x in (factor, inverses)]
    return call(body, outs + (held if keep else []), scalars, arrays, scratch, far=2)


def fold_more(scalars, own, inverses, spans):
    _, half, full = own.shape
    total = sum(count for _, _, count in spans)
    used = sorted({level for level, _, _ in spans})

    def body(s, w, own_ref, inv_ref, out_ref, folded_ref):
        for i, level in enumerate(used):
            folded_ref[i] = masked_inverse(inv_ref[level], s[3 + level])
        cursor = 0
        for level, at, count in spans:
            flat = own_ref[pl.ds(at, count)].reshape(count * half, full)
            product = dot(flat, folded_ref[used.index(level)]).reshape(count, half, full)
            for p in range(count):
                out_ref[cursor + p] = (product[p] * w[at + p].astype(F32)).astype(BF16)
            cursor += count

    outs = [((total, half, full), BF16)]
    scratch = [pltpu.VMEM((len(used), full, full), BF16)]
    return call(body, outs, scalars, [own, inverses], scratch)


def skip_level(scalars, upper, lower_mine, lower_theirs, direct, at):
    count, half, full = upper[0].shape
    n, chips = len(upper), len(lower_mine)

    def body(s, *refs):
        upper_refs, mine = refs[:n], refs[n : n + chips]
        theirs, folded_ref, out_ref, lower_ref = refs[n + chips :]
        chip, core, leaf = s[0], s[1], s[2]
        total = jnp.zeros((count * half, full), F32)
        for k in range(n):
            p = (leaf ^ k) & (n - 1)
            for q in range(chips):
                place = (chip ^ q) * 2
                lower_ref[k, pl.ds(aligned(place + core, half), half), :] = mine[q][p]
                lower_ref[k, pl.ds(aligned(place + 1 - core, half), half), :] = theirs[q, p]
            total = total + dot(upper_refs[k][...].reshape(count * half, full), lower_ref[k])
        direct = folded_ref[pl.ds(at, count)].astype(F32)
        out_ref[...] = (direct - total.reshape(count, half, full)).astype(BF16)

    outs = [((count, half, full), BF16)]
    arrays = [*upper, *lower_mine, lower_theirs, direct]
    return call(body, outs, scalars[:1], arrays, [pltpu.VMEM((n, full, full), BF16)])


def push(scalars, parts, full, group, pending, pair, at):
    rows, columns = parts[0].shape
    half = rows // 2
    n_parts = len(parts)
    n_pend = 0 if pending is None else 1

    def body(s, *refs):
        part_refs, m_refs = refs[:n_parts], refs[n_parts : n_parts + 2]
        pend_ref = refs[n_parts + 2] if n_pend else None
        outs, x_ref, all_ref = refs[n_parts + 2 + n_pend : -2], *refs[-2:]
        chip, core, leaf = s[0], s[1], s[2]
        for k in range(n_parts):
            x_ref[pl.ds(aligned(chip ^ k, rows), rows), :] = part_refs[k][...]
        for side in range(2):
            flat = m_refs[side][pl.ds(at, group)].reshape(group * half, full)
            all_ref[side] = dot(flat, x_ref[...]).reshape(group, half, columns)
        for k in range(group):
            p = (leaf ^ k) & (group - 1)
            for side, who in enumerate((core, 1 - core)):
                place = pl.ds(aligned(who, half), half)
                total = all_ref[side, p]
                if n_pend:
                    total = total + pend_ref[p, place, :]
                outs[k][place, :] = total.astype(outs[k].dtype)

    outs = [((rows, columns), BF16 if k else F32) for k in range(group)]
    arrays = [*parts, *pair, *([pending] if n_pend else [])]
    scratch = [
        pltpu.VMEM((full, columns), BF16),
        pltpu.VMEM((2, group, half, columns), F32),
    ]
    return call(body, outs, scalars[:1], arrays, scratch)


def finish(scalars, level, parts, inverses, sides, spans, pendings):
    rows, columns = parts[0].shape
    full = inverses.shape[1]
    half = rows // 2
    n, n_parts = len(spans), len(parts)
    n_s = 2 if n else 0
    fresh = pendings is None

    def body(s, w, *refs):
        part_refs, inv_ref = refs[:n_parts], refs[n_parts]
        refs = refs[n_parts + 1 :]
        side_refs, p_refs = refs[:n_s], refs[n_s : n_s + (0 if fresh else n)]
        outs, x_ref, turned_ref, y_ref = refs[n_s + (0 if fresh else n) : -3], *refs[-3:]
        chip, core, width = s[0], s[1], s[3 + level]
        for k in range(n_parts):
            x_ref[pl.ds(aligned(chip ^ k, rows), rows), :] = part_refs[k][...]
        keep = lax.broadcasted_iota(jnp.int32, (full, columns), 0) < width
        x = jnp.where(keep, x_ref[...], jnp.zeros((), BF16))
        y = jnp.where(keep, dot(inv_ref[level], x), 0.0).astype(BF16)
        y_ref[...] = y
        turned_ref[...] = jnp.where(keep, dot(y.T, inv_ref[level]).T, 0.0)
        outs[0][...] = turned_ref[pl.ds(aligned(chip, rows), rows), :]
        for at, who in ((1, core), (2, 1 - core)):
            outs[at][...] = y_ref[pl.ds(aligned(chip * 2 + who, half), half), :]
        for k, (at, count) in enumerate(spans):
            for side, who in enumerate((core, 1 - core)):
                place = pl.ds(aligned(who, half), half)
                product = dot(side_refs[side][pl.ds(at, count)].reshape(count * half, full), y)
                product = product.reshape(count, half, columns)
                for p in range(count):
                    term = product[p] * w[at + p].astype(F32)
                    if not fresh:
                        term = term + p_refs[k][p, place, :]
                    outs[3 + k][p, place, :] = term

    outs = [((rows, columns), F32), ((half, columns), BF16), ((half, columns), BF16)]
    outs += [((count, rows, columns), F32) for _, count in spans]
    arrays = [*parts, inverses, *(sides if n else []), *([] if fresh else pendings)]
    scratch = [
        pltpu.VMEM((full, columns), BF16),
        pltpu.VMEM((full, columns), F32),
        pltpu.VMEM((full, columns), BF16),
    ]
    return call(body, outs, scalars, arrays, scratch)


def two_sides(stack_ref, piece_refs, vector, leaf, core, weights=None):
    count = len(vector)
    half = piece_refs[0].shape[1] // 2
    for k, (array, slot) in enumerate(vector):
        p = (leaf ^ k) & (count - 1)
        for side, who in enumerate((core, 1 - core)):
            piece = piece_refs[array][slot, pl.ds(aligned(who, half), half), :]
            if weights is not None:
                w, start = weights
                piece = (piece.astype(F32) * w[start + p].astype(F32)).astype(BF16)
            stack_ref[side, pl.ds(aligned(p, half), half), :] = piece
    return [stack_ref[side, : count * half, :].T for side in range(2)]


def pull(scalars, pieces, vectors, outputs, pairs, full, chips):
    _, rows, columns = pieces[0].shape
    half = rows // 2
    n_p, n_m = len(pieces), 2 * len(pairs)
    sums = [total for _, total in outputs if total is not None]
    tall = max(len(v) for v in vectors) * half

    def body(s, *refs):
        piece_refs, m_refs = refs[:n_p], refs[n_p : n_p + n_m]
        waiting = list(refs[n_p + n_m : n_p + n_m + len(sums)])
        outs, stack_ref, turned_ref = refs[n_p + n_m + len(sums) : -2], *refs[-2:]
        chip, core, leaf = s[0], s[1], s[2]
        lefts = [
            two_sides(stack_ref.at[i], piece_refs, v, leaf, core) for i, v in enumerate(vectors)
        ]
        for slot, (terms, total) in enumerate(outputs):
            now = None if total is None else waiting.pop(0)[...]
            for v, which, at in terms:
                count = len(vectors[v])
                for side in range(2):
                    flat = m_refs[2 * which + side][pl.ds(at, count)].reshape(count * half, full)
                    product = dot(lefts[v][side], flat)
                    now = product if now is None else now + product
            turned_ref[slot] = now.T
            for k in range(chips):
                block = turned_ref[slot, pl.ds(aligned(chip ^ k, rows), rows), :]
                outs[k][slot] = block.astype(outs[k].dtype)

    outs = [((len(outputs), rows, columns), BF16 if k else F32) for k in range(chips)]
    arrays = [*pieces, *[m for pair in pairs for m in pair], *sums]
    scratch = [
        pltpu.VMEM((len(vectors), 2, tall, columns), BF16),
        pltpu.VMEM((len(outputs), full, columns), F32),
    ]
    return call(body, outs, scalars[:1], arrays, scratch)


def pull_rest(scalars, pieces, vectors, outputs, sides, inverses):
    _, rows, columns = pieces[0].shape
    half = rows // 2
    full = inverses.shape[1]
    n_p = len(pieces)
    sums = [o[2] for o in outputs if o[2] is not None]
    tall = max(len(v) for v in vectors) * half
    n_terms = sum(len(terms) for _, terms, _, _ in outputs)

    def body(s, w, *refs):
        piece_refs, side_refs, inv_ref = refs[:n_p], refs[n_p : n_p + 2], refs[n_p + 2]
        waiting = list(refs[n_p + 3 : n_p + 3 + len(sums)])
        outs, stack_ref = refs[n_p + 3 + len(sums) : -1], refs[-1]
        core, leaf = s[1], s[2]
        place = 0
        for slot, (level, terms, total, complete) in enumerate(outputs):
            now = None if total is None else waiting.pop(0)[...]
            for v, at in terms:
                count = len(vectors[v])
                lefts = two_sides(
                    stack_ref.at[place], piece_refs, vectors[v], leaf, core, (w, at)
                )
                place += 1
                for side in range(2):
                    flat = side_refs[side][pl.ds(at, count)].reshape(count * half, full)
                    product = dot(lefts[side], flat)
                    now = product if now is None else now + product
            if complete:
                keep = lax.broadcasted_iota(jnp.int32, (columns, full), 1) < s[3 + level]
                now = jnp.where(keep, now, 0.0).astype(BF16)
                now = jnp.where(keep, dot(now, inv_ref[level]), 0.0)
            outs[slot][...] = now

    outs = [((columns, full), F32)] * len(outputs)
    arrays = [*pieces, *sides, inverses, *sums]
    return call(body, outs, scalars, arrays, [pltpu.VMEM((n_terms, 2, tall, columns), BF16)])


def shards(rhs, diag_inverse, factor, widths, structure):
    leaf_count = lax.axis_size("leaf")
    chips = lax.axis_size("row") // 2
    leaf = lax.axis_index("leaf")
    row = lax.axis_index("row")
    chip, core = row // 2, row % 2
    levels, block_rows = rhs.shape[0], rhs.shape[2]
    half, full = rhs.shape[3] // 2, factor.shape[3]
    first = core == 0
    offsets = block_offsets(levels, leaf_count)
    group = [group_size(l, leaf_count) for l in range(levels)]
    top, mid, low = levels - 1, levels - 2, levels - 3

    def in_order(mine, theirs, axis):
        return jnp.where(
            first,
            jnp.concatenate([mine, theirs], axis),
            jnp.concatenate([theirs, mine], axis),
        )

    def exchange(pieces, axis, scale, order):
        taken = {}
        for k in order:
            taken[k] = from_partner(pieces[k - 1], axis, scale * k)
        return [taken[k] for k in sorted(taken)]

    def exchange_chips(pieces):
        return exchange(pieces, "row", 2, chip_order(len(pieces)))

    def exchange_leaves(pieces):
        return exchange(pieces, "leaf", 1, leaf_order(len(pieces)))

    def gather_chips(stacked):
        return [stacked] + exchange_chips([stacked] * (chips - 1))

    left_half, right_half = rhs[:, 0, :, :half], rhs[:, 0, :, half:]
    rhs_theirs = from_partner(jnp.where(first, right_half, left_half), "row", 1)
    rhs_pair = in_order(jnp.where(first, left_half, right_half), rhs_theirs, 1)
    places = jnp.stack([chip, core, leaf]).astype(jnp.int32)
    scalars = [jnp.concatenate([places, widths[:, 0]]), structure[0]]

    folded_at = {}

    def spans_of(pairs):
        cursor, spans = 0, []
        for s, t in pairs:
            folded_at[s, t] = cursor
            spans.append((s, offsets[s, t], group[t]))
            cursor += group[t]
        return spans

    def swap(mine):
        return mine, from_partner(mine, "row", 1)

    def fold(pairs, picked, blocks, levels, keep):
        places = [pairs.index(pair) for pair in picked]
        mine, *others = fold_blocks(scalars, factor[0], diag_inverse[0], spans_of(pairs), places, blocks, levels, keep)
        return swap(mine), others[: len(picked)], others[len(picked) :]

    lowest = [(0, 1), (0, 2)]
    folded_first, (lower_half,), _ = fold(lowest, [(0, 1)], group[1] + group[2], 1, False)
    others = [(s, s + 1) for s in range(1, top)]
    folded, (upper_half, high_lower, high_upper), (own_blocks, inverses) = fold(
        others, [(1, 2), (low, mid), (mid, top)], factor.shape[1], levels, True
    )
    late = sorted([(s, t) for s in range(1, low) for t in (low, mid) if t > s + 1] + [(low, top)])
    (late_mine,) = fold_more(scalars, own_blocks, inverses, spans_of(late))
    folded_late = swap(late_mine)
    their_blocks = from_partner(factor[0], "row", 1)
    sides = [own_blocks, their_blocks]

    def spread(piece, cuts):
        gathered = [piece]
        for k in range(1, chips):
            count = piece.shape[0] // cuts[k]
            got = []
            for i in range(cuts[k]):
                got.append(from_partner(piece[i * count : (i + 1) * count], "row", 2 * k))
            gathered.append(got[0] if len(got) == 1 else jnp.concatenate(got))
        return gathered

    lower_mine = spread(lower_half, cuts_of(chips, 1))
    upper = [upper_half] + exchange_leaves([upper_half] * (group[1] - 1))
    high_mine = spread(high_lower, cuts_of(chips, CUTS))
    high = [high_upper] + exchange_leaves([high_upper] * (leaf_count - 1))

    def skip_product(upper, lower_mine, direct, at, after):
        upper, lower_mine, _ = lax.optimization_barrier((upper, lower_mine, after))
        lower_theirs = from_partner(jnp.stack(lower_mine), "row", 1)
        (mine,) = skip_level(scalars, upper, lower_mine, lower_theirs, direct, at)
        return swap(mine)

    pending = {t: None for t in range(levels)}
    turned, kept, sent = [None] * levels, [None] * levels, [None] * levels

    def finish_level(l, parts):
        later = list(range(l + 2, levels))
        before = None if l == 0 else [pending[t] for t in later]
        spans = [(offsets[l, t], group[t]) for t in later]
        turned[l], kept[l], sent[l], *after = finish(
            scalars, l, parts, inverses, sides, spans, before
        )
        pending.update(zip(later, after))

    def push_level(l, parts):
        pair, at = folded if l else folded_first, folded_at[l, l + 1]
        return push(scalars, parts, full, group[l + 1], pending[l + 1], pair, at)

    parts = gather_chips(rhs_pair[0])
    own, *messages = push_level(0, parts)
    for l in range(1, levels):
        received = exchange_leaves(messages)
        finish_level(l - 1, parts)
        update = own
        for piece in received:
            update = update + piece.astype(F32)
        now = (rhs_pair[l].astype(F32) - update).astype(BF16)
        parts = gather_chips(now)
        if l < top:
            own, *messages = push_level(l, parts)
    high_skip = skip_product(high, high_mine, late_mine, folded_at[low, top], own)
    finish_level(top, parts)

    adjoint = [None] * levels

    def gather_leaves(named):
        span = max(group[l] for l, _ in named)
        listed = [[i for i, (l, _) in enumerate(named) if group[l] > k] for k in range(span)]
        stacks = [jnp.stack([named[i][1] for i in row]) for row in listed]
        pieces = [stacks[0]] + exchange_leaves(stacks[1:])
        vectors = [
            [(k, listed[k].index(i)) for k in range(group[l])] for i, (l, _) in enumerate(named)
        ]
        return pieces, vectors

    def total_of(own, received, slot):
        total = own[slot]
        for piece in received:
            total = total + piece[slot].astype(F32)
        return total

    adjoint[top] = turned[top].astype(BF16)
    pieces, vectors = gather_leaves([(top, adjoint[top]), (mid, turned[mid].astype(BF16))])
    outputs = [
        ([(0, 1, 0), (1, 0, folded_at[low, mid])], None),
        ([(0, 0, folded_at[mid, top])], None),
    ]
    own, *messages = pull(scalars, pieces, vectors, outputs, [folded, high_skip], full, chips)
    received = exchange_chips(messages)
    listed = [(s, [(0, offsets[s, top])], None, s > 0) for s in range(low)]
    sums = dict(enumerate(pull_rest(scalars, pieces, vectors[:1], listed, sides, inverses)))
    adjoint[low] = (turned[low] - total_of(own, received, 0)).astype(BF16)
    adjoint[mid] = (turned[mid] - total_of(own, received, 1)).astype(BF16)
    uppers = [low, mid]
    pieces, vectors = gather_leaves([(t, adjoint[t]) for t in uppers])
    for l in range(low - 1, 1, -1):

        def term(s, i, t):
            return (i, 0, folded_at[s, t]) if t == s + 1 else (i, 1, folded_at[s, t])

        lower = [l, 1] if l == 2 else [l]
        outputs = [([term(s, i, t) for i, t in enumerate(uppers)], sums[s]) for s in lower]
        own, *messages = pull(scalars, pieces, vectors, outputs, [folded, folded_late], full, chips)
        received = exchange_chips(messages)
        if l == 2:
            skip = skip_product(upper, lower_mine, folded_first[0], folded_at[0, 2], own)
        left = [s for s in range(l) if s not in lower]
        listed = [
            (s, [(i, offsets[s, t]) for i, t in enumerate(uppers)], sums[s], l == 2) for s in left
        ]
        sums.update(zip(left, pull_rest(scalars, pieces, vectors, listed, sides, inverses)))
        adjoint[l] = (turned[l] - total_of(own, received, 0)).astype(BF16)
        named = [(l, adjoint[l])]
        if l == 2:
            ahead = turned[1] - total_of(own, received, 1)
            named.append((1, ahead.astype(BF16)))
        uppers = [l]
        pieces, vectors = gather_leaves(named)
    outputs = [
        ([(0, 1, 0), (1, 2, folded_at[0, 1])], sums[0]),
        ([(0, 0, folded_at[1, 2])], None),
    ]
    own, *messages = pull(scalars, pieces, vectors, outputs, [folded, skip, folded_first], full, chips)
    received = exchange_chips(messages)
    adjoint[0] = (turned[0] - total_of(own, received, 0)).astype(BF16)
    adjoint[1] = (ahead - total_of(own, received, 1)).astype(BF16)

    theirs = from_partner(jnp.stack(sent), "row", 1)
    forward = in_order(jnp.stack(kept), theirs, 2)

    def swap_rows(values):
        stacked = jnp.stack(values)
        low_rows, high_rows = stacked[:, :block_rows], stacked[:, block_rows:]
        theirs = from_partner(jnp.where(first, high_rows, low_rows), "row", 1)
        return in_order(jnp.where(first, low_rows, high_rows), theirs, 2)

    upper_levels = swap_rows(adjoint[2:])
    backward = jnp.concatenate([swap_rows(adjoint[:2]), upper_levels])
    return forward[:, None], backward[:, None]


def cuts_of(chips, most):
    return [most if k >= chips // 2 else 1 for k in range(chips)]


def solution(mesh):
    placed = (
        P(None, "leaf", "row", None),
        P("leaf", None, None, None),
        P("leaf", None, "row", None),
        P(None, "leaf"),
        P("leaf", None),
    )

    def solve(rhs, diag_inverse, factor, widths, structure):
        step = jax.shard_map(
            shards,
            mesh=mesh,
            in_specs=placed,
            out_specs=(P(None, "leaf", "row", None), P(None, "leaf", "row", None)),
            check_vma=False,
        )
        return step(
            rhs, diag_inverse, factor, widths, structure
        )

    return solve
```
